256 devices in a mesh: tgt: 32 (over z_hi, y, x), lat: 8 (over z_lo, core).
Axes of the slice: x: 4, y: 4, z: 8 (z_hi: 2, z_lo: 4; z = z_hi * 4 + z_lo), core: 2. Of those that a mesh axis runs over, the one named last changes fastest.
Arguments:
- code_index: int32 [2, 512, 64], P(None, 'tgt'), may hold values from 0 to 16383, all different within a row
- code_value: bfloat16 [2, 512, 64], P(None, 'tgt'), may hold values from 0.5 to 4
- decoder: bfloat16 [2, 16384, 28672], P(None, 'lat', 'tgt'), may hold values from -0.25 to 0.25
- mlp_out: bfloat16 [512, 28672], P('lat', 'tgt'), may hold values from -6 to 6
Outputs:
- error: float32 [512, 28672], P('lat', 'tgt')
- code_grad: float32 [2, 512, 64], P(None, ('tgt', 'lat'))
The draws below stay inside these ranges and needn't reach their ends.
Inputs may be any that keep to these rules, and one draw needn't show every extreme that they name: `code_index`: within one source layer, the 64 latent numbers of a token are all different.
All inputs are finite; a program needn't handle non-finite values.
Results may differ from the reference program's by a relative error of at most 0.0004.
Values may be sent and summed in bfloat16 or wider, within the bound.
No kernel may reach another device: no remote copies, remote signals or barrier semaphores. Data moves between devices by JAX's collectives and lax.ppermute only.
A program may use at most 64 MiB of HBM per device.

```python
import math
import jax
import jax.numpy as jnp
from jax import lax

D = 3584
LAT = 16384
SOURCES = 2
TARGETS = 8
ACTIVE = 64
TOKENS = 512


def level_of(key, dims, cuts, smallest, top_value):
    gain = 1.0
    for position, blocks in cuts:
        draws = jax.random.uniform(jax.random.fold_in(jax.random.fold_in(key, 6), position), (blocks,), jnp.float32, smallest / len(cuts), top_value / len(cuts))
        gain = gain * jnp.repeat(jnp.exp(draws), dims[position] // blocks).reshape((-1,) + (1,) * (len(dims) - 1 - position))
    return gain


def distinct(key, rows, count, top, lift):
    ranking = jax.random.permutation(jax.random.fold_in(key, 1), count)
    boost = ranking
    for power in range(3):
        boost = boost * boost // count
    boost = boost * lift // count
    chance = jax.random.randint(jax.random.fold_in(key, 2), (rows, count), 0, 4096) + boost
    sure = jax.random.permutation(jax.random.fold_in(key, 3), rows)[jnp.arange(count) % rows]
    chance = jnp.where(jnp.arange(rows)[:, None] == sure[None, :], 1 << 14, chance)
    merit = chance * count + jnp.arange(count)
    return lax.top_k(merit.astype(jnp.int32), top)[1].astype(jnp.int32)


def centred(own_key, extent, width, bound, pieces=(), kind=jnp.bfloat16):
    level = level_of(own_key, extent, pieces, -0.22, 0.18) if pieces else 1.0
    array = jax.random.normal(own_key, extent, jnp.float32) * width * level
    return jnp.minimum(jnp.maximum(array, -bound), bound).astype(kind)


def setup_inputs(seed: int = 0) -> dict:
    key_list = jax.random.split(jax.random.key(seed), 5)
    code_index = distinct(key_list[0], SOURCES * TOKENS, LAT, ACTIVE, 64).reshape((SOURCES, TOKENS, ACTIVE))
    code_value = jnp.clip(jnp.exp(math.log(4.0) - 2.0794415 * jax.random.uniform(key_list[1], (SOURCES, TOKENS, ACTIVE), jnp.float32) ** level_of(key_list[1], (SOURCES, TOKENS, ACTIVE), ((1, 32),), -0.2, 0.2)), 0.5, 4.0).astype(jnp.bfloat16)
    decoder = centred(key_list[2], (SOURCES, LAT, TARGETS * D), (SOURCES * ACTIVE * 4) ** -0.5, 0.25, ((1, 8), (2, 32)))
    mlp_out = centred(key_list[3], (TOKENS, TARGETS * D), 1.0, 6.0, ((0, 8), (1, 32)))
    return dict(code_index=code_index, code_value=code_value, decoder=decoder, mlp_out=mlp_out)


def reference(code_index, code_value, decoder, mlp_out):
    rows = jnp.arange(TOKENS, dtype=jnp.int32)[:, None]
    recon = jnp.zeros((TOKENS, TARGETS * D), jnp.float32)
    for source in range(SOURCES):
        codes = jnp.zeros((TOKENS, LAT), jnp.bfloat16).at[rows, code_index[source]].add(code_value[source])
        recon = recon + jnp.dot(codes, decoder[source], preferred_element_type=jnp.float32)
    error = recon - mlp_out.astype(jnp.float32)
    picked_all = []
    for source in range(SOURCES):
        dense_grad = jnp.dot(error, decoder[source].T, precision=lax.Precision.HIGHEST, preferred_element_type=jnp.float32)
        picked_all.append(jnp.take_along_axis(dense_grad, code_index[source], axis=1) / TARGETS)
    return error, jnp.stack(picked_all, axis=0)
```

```python
import jax
import jax.numpy as jnp
from jax import lax
from jax.experimental import pallas as pl
from jax.experimental.pallas import tpu as pltpu
from jax.sharding import PartitionSpec as P

TARGETS = 8
LO = 128
NT = (((1,), (1,)), ((), ()))


def tgt_shift(zh):
    return [(t, t ^ (zh << 4)) for t in range(32)]


def lat_xor(d):
    return [(i, i ^ d) for i in range(8)]


def decode_kernel(x_ref, w_hbm, mine_ref, theirs_ref, codes_ref, w_ref, acc_ref, sem):
    chunks = codes_ref.shape[0]
    per_source = chunks // 2
    width = per_source * LO
    lat = lax.axis_index("lat")
    core = lat % 2
    start = lat * width
    steps = 8
    rows_w = w_hbm.shape[0] // steps
    for i in range(steps):
        part = pl.ds(i * rows_w, rows_w)
        pltpu.make_async_copy(w_hbm.at[part], w_ref.at[part], sem.at[i]).start()

    half_lane = lax.broadcasted_iota(jnp.int32, (1, 128), 1) < 64
    row_hi = lax.broadcasted_iota(jnp.int32, (per_source * 8, 128), 0)
    row_lo = lax.broadcasted_iota(jnp.int32, (LO, 128), 0)

    def densify(b, carry):
        block = x_ref[b]
        local = block[0:16].astype(jnp.int32) - start
        inside = (local >= 0) & (local < width)
        hi = jnp.where(inside, (local >> 7) * 8, -1024)
        lo = local & (LO - 1)
        val = block[16:32]
        rolled = [pltpu.roll(a, 64, 1) for a in (hi, lo, val)]

        def pair(i, t, source):
            plain = (hi, lo, val)[i]
            turned = rolled[i]
            first, second = (plain, turned) if source == 0 else (turned, plain)
            return jnp.where(half_lane, first[t : t + 1], second[t + 1 : t + 2])

        yx = b // 2
        zh = b % 2
        token = pl.multiple_of(zh * 256 + yx * 16, 16)
        for source in range(2):
            halves = []
            for t0 in (0, 8):
                lhs, rhs = [], []
                for j in range(4):
                    t = t0 + 2 * j
                    slot = jnp.where(half_lane, 2 * j, 2 * j + 1)
                    key = pair(0, t, source) + slot
                    lhs.append(jnp.where(row_hi == key, pair(2, t, source), 0.0).astype(jnp.bfloat16))
                    rhs.append(jnp.where(row_lo == pair(1, t, source), 1.0, 0.0).astype(jnp.bfloat16))
                dense = lax.dot_general(
                    jnp.concatenate(lhs, axis=1),
                    jnp.concatenate(rhs, axis=1),
                    NT,
                    preferred_element_type=jnp.float32,
                )
                halves.append(dense.reshape(per_source, 8, LO))
            both = jnp.concatenate(halves, axis=1).astype(jnp.bfloat16)
            codes_ref[source * per_source : (source + 1) * per_source, pl.ds(token, 16), :] = both
        return carry

    lax.fori_loop(0, x_ref.shape[0], densify, 0)

    per_step = chunks // steps
    for i in range(steps):
        part = pl.ds(i * rows_w, rows_w)
        pltpu.make_async_copy(w_hbm.at[part], w_ref.at[part], sem.at[i]).wait()
        lhs = jnp.concatenate([codes_ref[i * per_step + j] for j in range(per_step)], axis=1)
        out = jnp.dot(lhs, w_ref[i * rows_w : (i + 1) * rows_w, :], preferred_element_type=jnp.float32)
        if i == 0:
            acc_ref[...] = out
        else:
            acc_ref[...] += out
    for z in range(4):
        mine_ref[z] = acc_ref[pl.ds(pl.multiple_of(z * 128 + core * 64, 64), 64), :]
        theirs_ref[z] = acc_ref[pl.ds(pl.multiple_of(z * 128 + (1 - core) * 64, 64), 64), :]


def decode(x, w):
    tokens, cols = 512, w.shape[1]
    part = jax.ShapeDtypeStruct((4, tokens // 8, cols), jnp.float32)
    return pl.pallas_call(
        decode_kernel,
        out_shape=(part, part),
        in_specs=[pl.BlockSpec(memory_space=pltpu.VMEM), pl.BlockSpec(memory_space=pl.ANY)],
        out_specs=(pl.BlockSpec(memory_space=pltpu.VMEM), pl.BlockSpec(memory_space=pltpu.VMEM)),
        scratch_shapes=[
            pltpu.VMEM((w.shape[0] // LO, tokens, LO), jnp.bfloat16),
            pltpu.VMEM(w.shape, jnp.bfloat16),
            pltpu.VMEM((tokens, cols), jnp.float32),
            pltpu.SemaphoreType.DMA((8,)),
        ],
        compiler_params=pltpu.CompilerParams(vmem_limit_bytes=48 << 20),
        name="decode",
    )(x, w)


def grads_kernel(x_ref, *refs):
    blocks = refs[:8]
    w_ref, out_ref, err_ref, key_ref, lo_ref = refs[8:]
    step = pl.program_id(0)
    per_step = w_ref.shape[0] // LO
    per_source = per_step * pl.num_programs(0) // 2
    tokens = out_ref.shape[0]
    lat = lax.axis_index("lat")

    @pl.when(step == 0)
    def _():
        core = lat % 2
        z = lat // 2
        for n, ref in enumerate(blocks):
            d, side = n % 4, n // 4
            c = core if side == 0 else 1 - core
            row = pl.multiple_of((z ^ d) * 128 + c * 64, 64)
            e = ref[...]
            high = e.astype(jnp.bfloat16)
            err_ref[pl.ds(row, 64), :] = high
            err_ref[pl.ds(pl.multiple_of(tokens + row, 64), 64), :] = (e - high.astype(jnp.float32)).astype(jnp.bfloat16)
        width = per_source * LO
        source = lax.broadcasted_iota(jnp.int32, (16, 128), 1) // 64
        for b in range(32):
            local = x_ref[b, 0:16, :].astype(jnp.int32) - lat * width
            inside = (local >= 0) & (local < width)
            row = (b % 2) * 256 + (b // 2) * 16
            key_ref[row : row + 16, :] = jnp.where(inside, (local >> 7) + source * per_source, -1)
            lo_ref[row : row + 16, :] = local & (LO - 1)
        out_ref[...] = jnp.zeros_like(out_ref)

    grads = lax.dot_general(err_ref[...], w_ref[...], NT, preferred_element_type=jnp.float32)
    grads = grads[:tokens] + grads[tokens:]
    key = key_ref[...]
    lo = lo_ref[...]
    picked = out_ref[...]
    for j in range(per_step):
        found = jnp.take_along_axis(grads[:, j * LO : (j + 1) * LO], lo, axis=1)
        picked = jnp.where(key == step * per_step + j, found, picked)
    out_ref[...] = picked


def grads(x, blocks, w):
    tokens, cols = 512, w.shape[1]
    tile = 256
    whole = lambda a: pl.BlockSpec(a.shape, lambda i: (0,) * a.ndim)
    return pl.pallas_call(
        grads_kernel,
        out_shape=jax.ShapeDtypeStruct((tokens, 128), jnp.float32),
        grid=(w.shape[0] // tile,),
        in_specs=[whole(x)] + [whole(b) for b in blocks] + [pl.BlockSpec((tile, cols), lambda i: (i, 0))],
        out_specs=pl.BlockSpec((tokens, 128), lambda i: (0, 0)),
        scratch_shapes=[
            pltpu.VMEM((2 * tokens, cols), jnp.bfloat16),
            pltpu.VMEM((tokens, 128), jnp.int32),
            pltpu.VMEM((tokens, 128), jnp.int32),
        ],
        compiler_params=pltpu.CompilerParams(vmem_limit_bytes=48 << 20),
        name="grads",
    )(x, *blocks, w)


def body(code_index, code_value, decoder, mlp_out):
    sources, lat_width, cols = decoder.shape
    w = decoder.reshape(sources * lat_width, cols)
    rows = code_index.shape[1]
    lat = lax.axis_index("lat")
    z = lat // 2
    zh = lax.axis_index("tgt") // 16

    index = jnp.transpose(code_index, (1, 0, 2)).reshape(rows, 128).astype(jnp.float32)
    value = jnp.transpose(code_value, (1, 0, 2)).reshape(rows, 128).astype(jnp.float32)
    own = jnp.concatenate([index, value], axis=0)
    other = lax.ppermute(own, "tgt", tgt_shift(1))
    both = jnp.where(zh == 0, jnp.stack([own, other]), jnp.stack([other, own]))
    groups = [[a * 16 + i for i in range(16)] for a in range(2)]
    sent = jnp.broadcast_to(both[None], (16,) + both.shape).reshape(32, 2 * rows, 128)
    x = lax.all_to_all(sent, "tgt", 0, 0, tiled=True, axis_index_groups=groups)

    mine, theirs = decode(x, w)
    chip = mine + lax.ppermute(theirs, "lat", lat_xor(1))
    near = [
        lax.ppermute(lax.dynamic_index_in_dim(chip, z ^ d, 0, keepdims=False), "lat", lat_xor(2 * d))
        for d in (1, 2, 3)
    ]
    error = lax.dynamic_index_in_dim(chip, z, 0, keepdims=False) + near[0] + near[1] + near[2]
    error = error - mlp_out.astype(jnp.float32)

    blocks = [error] + [lax.ppermute(error, "lat", lat_xor(2 * d)) for d in (1, 2, 3)]
    blocks = blocks + [lax.ppermute(b, "lat", lat_xor(1)) for b in blocks]
    picked = grads(x, blocks, w)
    parts = lax.all_to_all(picked, ("tgt", "lat"), 0, 0, tiled=True)
    total = jnp.sum(parts.reshape(256, 2, sources, 64), axis=0)
    return (error, jnp.transpose(total, (1, 0, 2)) / TARGETS)


def solution(mesh):
    placed = (P(None, "tgt", None), P(None, "tgt", None), P(None, "lat", "tgt"), P("lat", "tgt"))
    return jax.shard_map(
        body,
        mesh=mesh,
        in_specs=placed,
        out_specs=(P("lat", "tgt"), P(None, ("tgt", "lat"), None)),
        check_vma=False,
    )
```

```python
import jax
import jax.numpy as jnp
from jax import lax
from jax.experimental import pallas as pl
from jax.experimental.pallas import tpu as pltpu
from jax.sharding import PartitionSpec as P

TARGETS = 8
PARTS = 1
LO = 128
NT = (((1,), (1,)), ((), ()))
VALUE_SCALE = 256.0
TOP = 32000.0
STEPS = 64.0
VMEM_SPEC = pl.BlockSpec(memory_space=pltpu.VMEM)
ANY_SPEC = pl.BlockSpec(memory_space=pl.ANY)
PARAMS = pltpu.CompilerParams(vmem_limit_bytes=40 << 20)


def tgt_shift(zh):
    return [(t, t ^ (zh << 4)) for t in range(32)]


def lat_xor(d):
    return [(i, i ^ d) for i in range(8)]


def start_weights(w_hbm, w_ref, sem, steps):
    rows = w_hbm.shape[0] // steps
    copies = []
    for i in range(steps):
        part = pl.ds(i * rows, rows)
        copies.append(pltpu.make_async_copy(w_hbm.at[part], w_ref.at[part], sem.at[i]))
        copies[-1].start()
    return copies


def encode(x):
    cols = x.shape[1] // 128
    parts = [x[:, c * 128 : (c + 1) * 128] for c in range(cols)]
    top = jnp.abs(parts[0])
    for p in parts[1:]:
        top = jnp.maximum(top, jnp.abs(p))
    level = jnp.ceil(jnp.log2(jnp.maximum(top, 1e-30)) * STEPS)
    inverse = jnp.exp2(level * (-1.0 / STEPS)) * TOP
    codes = [jnp.round(p * inverse).astype(jnp.int32).astype(jnp.int16) for p in parts]
    return jnp.concatenate(codes + [level.astype(jnp.int32).astype(jnp.int16)], axis=1)


def decoded(q):
    cols = q.shape[1] // 128 - 1
    wide = q.astype(jnp.int32).astype(jnp.float32)
    scale = jnp.exp2(wide[:, cols * 128 :] * (1.0 / STEPS)) * (1.0 / TOP)
    return jnp.concatenate([wide[:, c * 128 : (c + 1) * 128] * scale for c in range(cols)], axis=1)


def decode_kernel(part, x_ref, w_hbm, mine_ref, theirs_ref, codes_ref, w_ref, acc_ref, sem):
    chunks, tokens = codes_ref.shape[:2]
    his = chunks // 2
    width = his * LO
    group = tokens // 8
    blocks = group // 16
    lat = lax.axis_index("lat")
    core = lat % 2
    start = lat * width
    steps = 8
    rows_w = w_hbm.shape[0] // steps
    copies = start_weights(w_hbm, w_ref, sem, steps)

    half_lane = lax.broadcasted_iota(jnp.int32, (1, 128), 1) < 64
    shape = (his * 8 // 16, 16, 128)
    rows = lax.broadcasted_iota(jnp.int32, shape, 0) * 16 + lax.broadcasted_iota(jnp.int32, shape, 1)
    rows = rows.astype(jnp.float32).astype(jnp.bfloat16)
    zero = jnp.zeros((), jnp.bfloat16)
    one = jnp.ones((), jnp.bfloat16)

    def densify(i, carry):
        zy = i // blocks
        xl = i % blocks
        y = zy % 4
        block = x_ref[(y * 4 + part * blocks + xl) * 2 + zy // 4].astype(jnp.int32)
        local = block[0:16] - start
        inside = (local >= 0) & (local < width)
        hi = jnp.where(inside, (local >> 7) * 8, -1024).astype(jnp.float32)
        lo = (local & (LO - 1)).astype(jnp.float32)
        val = block[16:32].astype(jnp.float32) * (1.0 / VALUE_SCALE)
        both = [(a, pltpu.roll(a, 64, 1)) for a in (hi, lo, val)]

        def pair(n, t, source, extra=None):
            first, second = both[n] if source == 0 else both[n][::-1]
            row = jnp.where(half_lane, first[t : t + 1], second[t + 1 : t + 2])
            if extra is not None:
                row = row + extra
            return jnp.broadcast_to(row, (16, 128)).astype(jnp.bfloat16)[None]

        row = pl.multiple_of(i * 16, 16)
        for source in range(2):
            halves = []
            for t0 in (0, 8):
                lhs, rhs = [], []
                for j in range(4):
                    t = t0 + 2 * j
                    slot = jnp.where(half_lane, 2.0 * j, 2.0 * j + 1)
                    key = pair(0, t, source, slot)
                    lhs.append(jnp.where(rows == key, pair(2, t, source), zero).reshape(his * 8, 128))
                    rhs.append(jnp.where(rows == pair(1, t, source), one, zero).reshape(LO, 128))
                dense = lax.dot_general(
                    jnp.concatenate(lhs, axis=1),
                    jnp.concatenate(rhs, axis=1),
                    NT,
                    preferred_element_type=jnp.float32,
                )
                halves.append(dense.reshape(his, 8, LO))
            dense = jnp.concatenate(halves, axis=1).astype(jnp.bfloat16)
            codes_ref[source * his : (source + 1) * his, pl.ds(row, 16), :] = dense
        return carry

    lax.fori_loop(0, tokens // 16, densify, 0, unroll=8)

    per_step = chunks // steps
    for i in range(steps):
        copies[i].wait()
        lhs = jnp.concatenate([codes_ref[i * per_step + j] for j in range(per_step)], axis=1)
        out = jnp.dot(lhs, w_ref[i * rows_w : (i + 1) * rows_w, :], preferred_element_type=jnp.float32)
        if i == 0:
            acc_ref[...] = out
        else:
            acc_ref[...] += out
    for z in range(4):
        row = pl.multiple_of((z * 2 + core) * group, group)
        mine_ref[z] = acc_ref[pl.ds(row, group), :]
        row = pl.multiple_of((z * 2 + 1 - core) * group, group)
        theirs_ref[z] = acc_ref[pl.ds(row, group), :]


def decode(x, w, part):
    tokens, cols = 512 // PARTS, w.shape[1]
    shape = jax.ShapeDtypeStruct((4, tokens // 8, cols), jnp.float32)
    return pl.pallas_call(
        lambda *refs: decode_kernel(part, *refs),
        out_shape=(shape, shape),
        in_specs=[VMEM_SPEC, ANY_SPEC],
        out_specs=(VMEM_SPEC, VMEM_SPEC),
        scratch_shapes=[
            pltpu.VMEM((w.shape[0] // LO, tokens, LO), jnp.bfloat16),
            pltpu.VMEM(w.shape, jnp.bfloat16),
            pltpu.VMEM((tokens, cols), jnp.float32),
            pltpu.SemaphoreType.DMA((8,)),
        ],
        compiler_params=PARAMS,
        cost_estimate=pl.CostEstimate(
            flops=4 * tokens * w.shape[0] * cols, transcendentals=0, bytes_accessed=2 * w.size
        ),
        name=f"decode{part}",
    )(x, w)


def pack_kernel(mine_ref, recv_ref, own_ref, *near_refs):
    z = lax.axis_index("lat") // 2
    own_ref[...] = mine_ref[z] + recv_ref[z]
    for d in (1, 2, 3):
        near_refs[d - 1][...] = encode(mine_ref[z ^ d] + recv_ref[z ^ d])


def pack(mine, recv, part):
    _, rows, cols = mine.shape
    coded = jax.ShapeDtypeStruct((rows, cols + 128), jnp.int16)
    return pl.pallas_call(
        pack_kernel,
        out_shape=(jax.ShapeDtypeStruct((rows, cols), jnp.float32), coded, coded, coded),
        in_specs=[VMEM_SPEC] * 2,
        out_specs=(VMEM_SPEC,) * 4,
        compiler_params=PARAMS,
        name=f"pack{part}",
    )(mine, recv)


def error_kernel(part, own_ref, a_ref, b_ref, c_ref, mlp_ref, error_ref, code_ref):
    rows = own_ref.shape[0]
    total = own_ref[...] + decoded(a_ref[...]) + decoded(b_ref[...]) + decoded(c_ref[...])
    error = total - mlp_ref[part * rows : (part + 1) * rows, :].astype(jnp.float32)
    error_ref[...] = error
    code_ref[...] = encode(error)


def error_of(own, near, mlp, part):
    rows, cols = own.shape
    return pl.pallas_call(
        lambda *refs: error_kernel(part, *refs),
        out_shape=(
            jax.ShapeDtypeStruct((rows, cols), jnp.float32),
            jax.ShapeDtypeStruct((rows, cols + 128), jnp.int16),
        ),
        in_specs=[VMEM_SPEC] * 5,
        out_specs=(VMEM_SPEC,) * 2,
        compiler_params=PARAMS,
        name=f"error{part}",
    )(own, *near, mlp)


def grads_kernel(part, x_ref, *refs):
    coded = refs[:8]
    w_hbm, out_ref, err_ref, w_ref, sem = refs[8:]
    steps = 8
    rows_w = w_hbm.shape[0] // steps
    copies = start_weights(w_hbm, w_ref, sem, steps)
    tokens = out_ref.shape[0]
    group = tokens // 8
    blocks = group // 16
    lat = lax.axis_index("lat")
    core = lat % 2
    z = lat // 2
    for n, ref in enumerate(coded):
        d, side = n % 4, n // 4
        c = core if side == 0 else 1 - core
        row = pl.multiple_of(((z ^ d) * 2 + c) * group, group)
        e = decoded(ref[...])
        high = e.astype(jnp.bfloat16)
        err_ref[pl.ds(row, group), :] = high
        err_ref[pl.ds(pl.multiple_of(tokens + row, group), group), :] = (e - high.astype(jnp.float32)).astype(
            jnp.bfloat16
        )
    chunks = w_hbm.shape[0] // LO
    his = chunks // 2
    width = his * LO
    source = lax.broadcasted_iota(jnp.int32, (16, 128), 1) // 64
    keys, los = [], []
    for i in range(tokens // 16):
        zy = i // blocks
        b = ((zy % 4) * 4 + part * blocks + i % blocks) * 2 + zy // 4
        local = x_ref[b, 0:16, :].astype(jnp.int32) - lat * width
        inside = (local >= 0) & (local < width)
        keys.append(jnp.where(inside, (local >> 7) + source * his, -1))
        los.append(local & (LO - 1))
    key = jnp.concatenate(keys, axis=0)
    lo = jnp.concatenate(los, axis=0)
    picked = jnp.zeros(out_ref.shape, jnp.float32)
    for i in range(steps):
        copies[i].wait()
        grads = lax.dot_general(
            err_ref[...], w_ref[i * rows_w : (i + 1) * rows_w, :], NT, preferred_element_type=jnp.float32
        )
        grads = grads[:tokens] + grads[tokens:]
        for j in range(rows_w // LO):
            found = jnp.take_along_axis(grads[:, j * LO : (j + 1) * LO], lo, axis=1)
            picked = jnp.where(key == i * (rows_w // LO) + j, found, picked)
    out_ref[...] = picked


def grads(x, coded, w, part):
    tokens, cols = 512 // PARTS, w.shape[1]
    return pl.pallas_call(
        lambda *refs: grads_kernel(part, *refs),
        out_shape=jax.ShapeDtypeStruct((tokens, 128), jnp.float32),
        in_specs=[VMEM_SPEC] * 9 + [ANY_SPEC],
        out_specs=VMEM_SPEC,
        scratch_shapes=[
            pltpu.VMEM((2 * tokens, cols), jnp.bfloat16),
            pltpu.VMEM(w.shape, jnp.bfloat16),
            pltpu.SemaphoreType.DMA((8,)),
        ],
        compiler_params=PARAMS,
        cost_estimate=pl.CostEstimate(
            flops=4 * tokens * w.shape[0] * cols, transcendentals=0, bytes_accessed=2 * w.size
        ),
        name=f"grads{part}",
    )(x, *coded, w)


def body(code_index, code_value, decoder, mlp_out):
    sources, lat_width, cols = decoder.shape
    w = decoder.reshape(sources * lat_width, cols)
    rows = code_index.shape[1]
    zh = lax.axis_index("tgt") // 16

    value = (code_value.astype(jnp.float32) * VALUE_SCALE).astype(jnp.int32)
    own = jnp.stack([code_index, value]).astype(jnp.int16)
    own = jnp.transpose(own, (0, 2, 1, 3)).reshape(2 * rows, 128)
    other = lax.ppermute(own, "tgt", tgt_shift(1))
    both = jnp.where(zh == 0, jnp.stack([own, other]), jnp.stack([other, own]))
    groups = [[a * 16 + i for i in range(16)] for a in range(2)]
    sent = jnp.broadcast_to(both[None], (16,) + both.shape).reshape(32, 2 * rows, 128)
    x = lax.all_to_all(sent, "tgt", 0, 0, tiled=True, axis_index_groups=groups)

    errors, picks = [], []
    for part in range(PARTS):
        mine, theirs = decode(x, w, part)
        recv = lax.ppermute(theirs, "lat", lat_xor(1))
        own_sum, *near = pack(mine, recv, part)
        near = [lax.ppermute(near[d - 1], "lat", lat_xor(2 * d)) for d in (1, 2, 3)]
        error, coded = error_of(own_sum, near, mlp_out, part)
        errors.append(error)
        coded = [coded] + [lax.ppermute(coded, "lat", lat_xor(2 * d)) for d in (1, 2, 3)]
        coded = coded + [lax.ppermute(c, "lat", lat_xor(1)) for c in coded]
        picks.append(grads(x, coded, w, part).reshape(8, 64 // PARTS, 128))
    error = jnp.concatenate(errors, axis=0)
    picked = jnp.concatenate(picks, axis=1).reshape(512, 128)
    parts = lax.all_to_all(picked, ("tgt", "lat"), 0, 0, tiled=True)
    total = jnp.sum(parts.reshape(256, 2, sources, 64), axis=0)
    return (error, jnp.transpose(total, (1, 0, 2)) / TARGETS)


def solution(mesh):
    placed = (P(None, "tgt", None), P(None, "tgt", None), P(None, "lat", "tgt"), P("lat", "tgt"))
    return jax.shard_map(
        body,
        mesh=mesh,
        in_specs=placed,
        out_specs=(P("lat", "tgt"), P(None, ("tgt", "lat"), None)),
        check_vma=False,
    )
```

```python
import jax
import jax.numpy as jnp
from jax import lax
from jax.experimental import pallas as pl
from jax.experimental.pallas import tpu as pltpu
from jax.sharding import PartitionSpec as P

TARGETS = 8
PARTS = 2
LO = 128
NT = (((1,), (1,)), ((), ()))
VALUE_SCALE = 256.0
TOP = 32000.0
STEPS = 64.0
VMEM_SPEC = pl.BlockSpec(memory_space=pltpu.VMEM)
ANY_SPEC = pl.BlockSpec(memory_space=pl.ANY)
HBM_SPEC = pl.BlockSpec(memory_space=pltpu.HBM)
PARAMS = pltpu.CompilerParams(vmem_limit_bytes=40 << 20)


def tgt_shift(zh):
    return [(t, t ^ (zh << 4)) for t in range(32)]


def lat_xor(d):
    return [(i, i ^ d) for i in range(8)]


def start_weights(w_hbm, w_ref, sem, steps):
    rows = w_hbm.shape[0] // steps
    copies = []
    for i in range(steps):
        part = pl.ds(i * rows, rows)
        copies.append(pltpu.make_async_copy(w_hbm.at[part], w_ref.at[part], sem.at[i]))
        copies[-1].start()
    return copies


def encode(x):
    cols = x.shape[1] // 128
    parts = [x[:, c * 128 : (c + 1) * 128] for c in range(cols)]
    top = jnp.abs(parts[0])
    for p in parts[1:]:
        top = jnp.maximum(top, jnp.abs(p))
    level = jnp.ceil(jnp.log2(jnp.maximum(top, 1e-30)) * STEPS)
    inverse = jnp.exp2(level * (-1.0 / STEPS)) * TOP
    codes = [jnp.round(p * inverse).astype(jnp.int32).astype(jnp.int16) for p in parts]
    return jnp.concatenate(codes + [level.astype(jnp.int32).astype(jnp.int16)], axis=1)


def decoded(q):
    cols = q.shape[1] // 128 - 1
    wide = q.astype(jnp.int32).astype(jnp.float32)
    scale = jnp.exp2(wide[:, cols * 128 :] * (1.0 / STEPS)) * (1.0 / TOP)
    return jnp.concatenate([wide[:, c * 128 : (c + 1) * 128] * scale for c in range(cols)], axis=1)


def decode_kernel(part, x_ref, w_hbm, mine_ref, theirs_ref, codes_ref, w_ref, acc_ref, sem):
    chunks, tokens = codes_ref.shape[:2]
    his = chunks // 2
    width = his * LO
    group = tokens // 8
    blocks = group // 16
    lat = lax.axis_index("lat")
    core = lat % 2
    start = lat * width
    steps = 8
    rows_w = w_hbm.shape[0] // steps
    copies = start_weights(w_hbm, w_ref, sem, steps)

    half_lane = lax.broadcasted_iota(jnp.int32, (1, 128), 1) < 64
    shape = (his * 8 // 16, 16, 128)
    rows = lax.broadcasted_iota(jnp.int32, shape, 0) * 16 + lax.broadcasted_iota(jnp.int32, shape, 1)
    rows = rows.astype(jnp.float32).astype(jnp.bfloat16)
    zero = jnp.zeros((), jnp.bfloat16)
    one = jnp.ones((), jnp.bfloat16)

    def densify(i, carry):
        zy = i // blocks
        xl = i % blocks
        y = zy % 4
        block = x_ref[(y * 4 + part * blocks + xl) * 2 + zy // 4].astype(jnp.int32)
        local = block[0:16] - start
        inside = (local >= 0) & (local < width)
        hi = jnp.where(inside, (local >> 7) * 8, -1024).astype(jnp.float32)
        lo = (local & (LO - 1)).astype(jnp.float32)
        val = block[16:32].astype(jnp.float32) * (1.0 / VALUE_SCALE)
        both = [(a, pltpu.roll(a, 64, 1)) for a in (hi, lo, val)]

        def pair(n, t, source, extra=None):
            first, second = both[n] if source == 0 else both[n][::-1]
            row = jnp.where(half_lane, first[t : t + 1], second[t + 1 : t + 2])
            if extra is not None:
                row = row + extra
            return jnp.broadcast_to(row, (16, 128)).astype(jnp.bfloat16)[None]

        row = pl.multiple_of(i * 16, 16)
        for source in range(2):
            halves = []
            for t0 in (0, 8):
                lhs, rhs = [], []
                for j in range(4):
                    t = t0 + 2 * j
                    slot = jnp.where(half_lane, 2.0 * j, 2.0 * j + 1)
                    key = pair(0, t, source, slot)
                    lhs.append(jnp.where(rows == key, pair(2, t, source), zero).reshape(his * 8, 128))
                    rhs.append(jnp.where(rows == pair(1, t, source), one, zero).reshape(LO, 128))
                dense = lax.dot_general(
                    jnp.concatenate(lhs, axis=1),
                    jnp.concatenate(rhs, axis=1),
                    NT,
                    preferred_element_type=jnp.float32,
                )
                halves.append(dense.reshape(his, 8, LO))
            dense = jnp.concatenate(halves, axis=1).astype(jnp.bfloat16)
            codes_ref[source * his : (source + 1) * his, pl.ds(row, 16), :] = dense
        return carry

    lax.fori_loop(0, tokens // 16, densify, 0, unroll=8)

    per_step = chunks // steps
    for i in range(steps):
        copies[i].wait()
        lhs = jnp.concatenate([codes_ref[i * per_step + j] for j in range(per_step)], axis=1)
        out = jnp.dot(lhs, w_ref[i * rows_w : (i + 1) * rows_w, :], preferred_element_type=jnp.float32)
        if i == 0:
            acc_ref[...] = out
        else:
            acc_ref[...] += out
    for z in range(4):
        row = pl.multiple_of((z * 2 + core) * group, group)
        mine_ref[z] = acc_ref[pl.ds(row, group), :]
        row = pl.multiple_of((z * 2 + 1 - core) * group, group)
        theirs_ref[z] = acc_ref[pl.ds(row, group), :]


def decode(x, w, part, after):
    tokens, cols = 512 // PARTS, w.shape[1]
    shape = jax.ShapeDtypeStruct((4, tokens // 8, cols), jnp.float32)
    return pl.pallas_call(
        lambda x_ref, w_ref, *refs: decode_kernel(part, x_ref, w_ref, *refs[len(after) :]),
        out_shape=(shape, shape),
        in_specs=[VMEM_SPEC, HBM_SPEC] + [ANY_SPEC] * len(after),
        out_specs=(VMEM_SPEC, VMEM_SPEC),
        scratch_shapes=[
            pltpu.VMEM((w.shape[0] // LO, tokens, LO), jnp.bfloat16),
            pltpu.VMEM(w.shape, jnp.bfloat16),
            pltpu.VMEM((tokens, cols), jnp.float32),
            pltpu.SemaphoreType.DMA((8,)),
        ],
        compiler_params=PARAMS,
        cost_estimate=pl.CostEstimate(
            flops=4 * tokens * w.shape[0] * cols, transcendentals=0, bytes_accessed=2 * w.size
        ),
    )(x, w, *after)


def pack_kernel(mine_ref, recv_ref, own_ref, *near_refs):
    z = lax.axis_index("lat") // 2
    own_ref[...] = mine_ref[z] + recv_ref[z]
    for d in (1, 2, 3):
        near_refs[d - 1][...] = encode(mine_ref[z ^ d] + recv_ref[z ^ d])


def pack(mine, recv):
    _, rows, cols = mine.shape
    coded = jax.ShapeDtypeStruct((rows, cols + 128), jnp.int16)
    return pl.pallas_call(
        pack_kernel,
        out_shape=(jax.ShapeDtypeStruct((rows, cols), jnp.float32), coded, coded, coded),
        in_specs=[VMEM_SPEC] * 2,
        out_specs=(VMEM_SPEC,) * 4,
        compiler_params=PARAMS,
    )(mine, recv)


def error_kernel(part, own_ref, a_ref, b_ref, c_ref, mlp_ref, error_ref, code_ref):
    rows = own_ref.shape[0]
    total = own_ref[...] + decoded(a_ref[...]) + decoded(b_ref[...]) + decoded(c_ref[...])
    error = total - mlp_ref[part * rows : (part + 1) * rows, :].astype(jnp.float32)
    error_ref[...] = error
    code_ref[...] = encode(error)


def error_of(own, near, mlp, part):
    rows, cols = own.shape
    return pl.pallas_call(
        lambda *refs: error_kernel(part, *refs),
        out_shape=(
            jax.ShapeDtypeStruct((rows, cols), jnp.float32),
            jax.ShapeDtypeStruct((rows, cols + 128), jnp.int16),
        ),
        in_specs=[VMEM_SPEC] * 5,
        out_specs=(VMEM_SPEC,) * 2,
        compiler_params=PARAMS,
    )(own, *near, mlp)


def grads_kernel(part, x_ref, *refs):
    coded = refs[:8]
    w_ref, out_ref, err_ref = refs[8:]
    steps = 4
    rows_w = w_ref.shape[0] // steps
    cols = w_ref.shape[1]
    tokens = out_ref.shape[0]
    group = tokens // 8
    blocks = group // 16
    lat = lax.axis_index("lat")
    core = lat % 2
    z = lat // 2
    for n, ref in enumerate(coded):
        d, side = n % 4, n // 4
        c = core if side == 0 else 1 - core
        row = pl.multiple_of(((z ^ d) * 2 + c) * group, group)
        e = decoded(ref[...])
        high = e.astype(jnp.bfloat16)
        err_ref[pl.ds(row, group), :cols] = high
        err_ref[pl.ds(row, group), cols:] = (e - high.astype(jnp.float32)).astype(jnp.bfloat16)
    chunks = w_ref.shape[0] // LO
    his = chunks // 2
    width = his * LO
    source = lax.broadcasted_iota(jnp.int32, (16, 128), 1) // 64
    keys, los = [], []
    for i in range(tokens // 16):
        zy = i // blocks
        b = ((zy % 4) * 4 + part * blocks + i % blocks) * 2 + zy // 4
        local = x_ref[b, 0:16, :].astype(jnp.int32) - lat * width
        inside = (local >= 0) & (local < width)
        keys.append(jnp.where(inside, (local >> 7) + source * his, -1))
        los.append(local & (LO - 1))
    key = jnp.concatenate(keys, axis=0)
    lo = jnp.concatenate(los, axis=0)
    picked = jnp.zeros(out_ref.shape, jnp.float32)
    for i in range(steps):
        w = w_ref[i * rows_w : (i + 1) * rows_w, :]
        grads = lax.dot_general(
            err_ref[...], jnp.concatenate([w, w], axis=1), NT, preferred_element_type=jnp.float32
        )
        for j in range(rows_w // LO):
            found = jnp.take_along_axis(grads[:, j * LO : (j + 1) * LO], lo, axis=1)
            picked = jnp.where(key == i * (rows_w // LO) + j, found, picked)
    out_ref[...] = picked


def grads(x, coded, w, part, after):
    tokens, cols = 512 // PARTS, w.shape[1]
    return pl.pallas_call(
        lambda *refs: grads_kernel(part, *refs[:10], *refs[10 + len(after) :]),
        out_shape=jax.ShapeDtypeStruct((tokens, 128), jnp.float32),
        in_specs=[VMEM_SPEC] * 10 + [ANY_SPEC] * len(after),
        out_specs=VMEM_SPEC,
        scratch_shapes=[pltpu.VMEM((tokens, 2 * cols), jnp.bfloat16)],
        compiler_params=PARAMS,
        cost_estimate=pl.CostEstimate(
            flops=4 * tokens * w.shape[0] * cols, transcendentals=0, bytes_accessed=2 * w.size
        ),
    )(x, *coded, w, *after)


def shift_z(x, d):
    return lax.ppermute(x, "lat", lat_xor(2 * d))


def layer(code_index, code_value, decoder, mlp_out):
    sources, lat_width, cols = decoder.shape
    w = decoder.reshape(sources * lat_width, cols)
    rows = code_index.shape[1]
    zh = lax.axis_index("tgt") // 16

    value = (code_value.astype(jnp.float32) * VALUE_SCALE).astype(jnp.int32)
    own = jnp.stack([code_index, value]).astype(jnp.int16)
    own = jnp.transpose(own, (0, 2, 1, 3)).reshape(2 * rows, 128)
    other = lax.ppermute(own, "tgt", tgt_shift(1))
    both = jnp.where(zh == 0, jnp.stack([own, other]), jnp.stack([other, own]))
    groups = [[a * 16 + i for i in range(16)] for a in range(2)]
    sent = jnp.broadcast_to(both[None], (16,) + both.shape).reshape(32, 2 * rows, 128)
    x = lax.all_to_all(sent, "tgt", 0, 0, tiled=True, axis_index_groups=groups)

    near_of, own_of, after = [], [], []
    for part in range(PARTS):
        mine, theirs = decode(x, pltpu.with_memory_space_constraint(w, pltpu.HBM), part, after)
        recv = lax.ppermute(theirs, "lat", lat_xor(1))
        own_sum, *after = pack(mine, recv)
        own_of.append(own_sum)
        near_of.append([shift_z(after[d - 1], d) for d in (1, 2, 3)])
    errors, coded_of, picks = [], [], []
    for part in range(PARTS):
        error, coded = error_of(own_of[part], near_of[part], mlp_out, part)
        errors.append(error)
        coded_of.append([coded] + [shift_z(coded, d) for d in (1, 2, 3)])
    for part in range(PARTS):
        coded = coded_of[part]
        coded = coded + [lax.ppermute(c, "lat", lat_xor(1)) for c in coded]
        after = [coded_of[-1][0]] if part + 1 < PARTS else []
        picked = grads(x, coded, w, part, after)
        picks.append(picked.reshape(8, 64 // PARTS, 128))
    error = jnp.concatenate(errors, axis=0)
    picked = jnp.concatenate(picks, axis=1).reshape(512, 128)
    parts = lax.all_to_all(picked, ("tgt", "lat"), 0, 0, tiled=True)
    total = jnp.sum(parts.reshape(256, 2, sources, 64), axis=0)
    return (error, jnp.transpose(total, (1, 0, 2)) / TARGETS)


def solution(mesh):
    placed = (P(None, "tgt", None), P(None, "tgt", None), P(None, "lat", "tgt"), P("lat", "tgt"))
    return jax.shard_map(
        layer,
        mesh=mesh,
        in_specs=placed,
        out_specs=(P("lat", "tgt"), P(None, ("tgt", "lat"), None)),
        check_vma=False,
    )
```

```python
import jax
import jax.numpy as jnp
from jax import lax
from jax.experimental import pallas as pl
from jax.experimental.pallas import tpu as pltpu
from jax.sharding import PartitionSpec as P

TARGETS = 8
PARTS = 2
LO = 128
NT = (((1,), (1,)), ((), ()))
VALUE_SCALE = 256.0
TOP = 32000.0
STEPS = 64.0
VMEM_SPEC = pl.BlockSpec(memory_space=pltpu.VMEM)
ANY_SPEC = pl.BlockSpec(memory_space=pl.ANY)
HBM_SPEC = pl.BlockSpec(memory_space=pltpu.HBM)
PARAMS = pltpu.CompilerParams(vmem_limit_bytes=40 << 20)


def mirror():
    pairs = []
    for t in range(32):
        for i in range(8):
            pairs.append((t * 8 + i, (t ^ 16) * 8 + ((3 - i // 2) * 2 + i % 2)))
    return pairs


def lat_xor(d):
    return [(i, i ^ d) for i in range(8)]


def start_weights(w_hbm, w_ref, sem, steps):
    rows = w_hbm.shape[0] // steps
    copies = []
    for i in range(steps):
        part = pl.ds(i * rows, rows)
        copies.append(pltpu.make_async_copy(w_hbm.at[part], w_ref.at[part], sem.at[i]))
        copies[-1].start()
    return copies


def encode(x):
    cols = x.shape[1] // 128
    parts = [x[:, c * 128 : (c + 1) * 128] for c in range(cols)]
    top = jnp.abs(parts[0])
    for p in parts[1:]:
        top = jnp.maximum(top, jnp.abs(p))
    level = jnp.ceil(jnp.log2(jnp.maximum(top, 1e-30)) * STEPS)
    inverse = jnp.exp2(level * (-1.0 / STEPS)) * TOP
    codes = [jnp.round(p * inverse).astype(jnp.int32).astype(jnp.int16) for p in parts]
    return jnp.concatenate(codes + [level.astype(jnp.int32).astype(jnp.int16)], axis=1)


def decoded(q):
    cols = q.shape[1] // 128 - 1
    wide = q.astype(jnp.int32).astype(jnp.float32)
    scale = jnp.exp2(wide[:, cols * 128 :] * (1.0 / STEPS)) * (1.0 / TOP)
    return jnp.concatenate([wide[:, c * 128 : (c + 1) * 128] * scale for c in range(cols)], axis=1)


def own_rows(part):
    lat = lax.axis_index("lat")
    row = pl.multiple_of((lat // 2 % 2) * 128 + (lat % 2) * 64, 64)
    zh = lax.axis_index("tgt") // 16
    return row, lat // 4 == (zh + part) % 2


def decode_kernel(part, x_ref, w_hbm, mlp_hbm, mine_ref, theirs_ref, codes_ref, w_ref, mlp_ref, acc_ref, sem):
    chunks, tokens = codes_ref.shape[:2]
    his = chunks // 2
    width = his * LO
    group = tokens // 8
    lat = lax.axis_index("lat")
    core = lat % 2
    start = lat * width
    steps = 8
    rows_w = w_hbm.shape[0] // steps
    copies = start_weights(w_hbm, w_ref, sem, steps)
    mlp_copy = pltpu.make_async_copy(mlp_hbm, mlp_ref, sem.at[steps])
    mlp_copy.start()

    half_lane = lax.broadcasted_iota(jnp.int32, (1, 128), 1) < 64
    shape = (his * 8 // 16, 16, 128)
    rows = lax.broadcasted_iota(jnp.int32, shape, 0) * 16 + lax.broadcasted_iota(jnp.int32, shape, 1)
    rows = rows.astype(jnp.float32).astype(jnp.bfloat16)
    zero = jnp.zeros((), jnp.bfloat16)
    one = jnp.ones((), jnp.bfloat16)

    def densify(i, carry):
        block = x_ref[i].astype(jnp.int32)
        local = block[0:16] - start
        inside = (local >= 0) & (local < width)
        hi = jnp.where(inside, (local >> 7) * 8, -1024).astype(jnp.float32)
        lo = (local & (LO - 1)).astype(jnp.float32)
        val = block[16:32].astype(jnp.float32) * (1.0 / VALUE_SCALE)
        both = [(a, pltpu.roll(a, 64, 1)) for a in (hi, lo, val)]

        def pair(n, t, source, extra=None):
            first, second = both[n] if source == 0 else both[n][::-1]
            row = jnp.where(half_lane, first[t : t + 1], second[t + 1 : t + 2])
            if extra is not None:
                row = row + extra
            return jnp.broadcast_to(row, (16, 128)).astype(jnp.bfloat16)[None]

        row = pl.multiple_of(i * 16, 16)
        for source in range(2):
            halves = []
            for t0 in (0, 8):
                lhs, rhs = [], []
                for j in range(4):
                    t = t0 + 2 * j
                    slot = jnp.where(half_lane, 2.0 * j, 2.0 * j + 1)
                    key = pair(0, t, source, slot)
                    lhs.append(jnp.where(rows == key, pair(2, t, source), zero).reshape(his * 8, 128))
                    rhs.append(jnp.where(rows == pair(1, t, source), one, zero).reshape(LO, 128))
                dense = lax.dot_general(
                    jnp.concatenate(lhs, axis=1),
                    jnp.concatenate(rhs, axis=1),
                    NT,
                    preferred_element_type=jnp.float32,
                )
                halves.append(dense.reshape(his, 8, LO))
            dense = jnp.concatenate(halves, axis=1).astype(jnp.bfloat16)
            codes_ref[source * his : (source + 1) * his, pl.ds(row, 16), :] = dense
        return carry

    lax.fori_loop(0, tokens // 16, densify, 0, unroll=8)

    per_step = chunks // steps
    for i in range(steps):
        copies[i].wait()
        lhs = jnp.concatenate([codes_ref[i * per_step + j] for j in range(per_step)], axis=1)
        out = jnp.dot(lhs, w_ref[i * rows_w : (i + 1) * rows_w, :], preferred_element_type=jnp.float32)
        if i == 0:
            acc_ref[...] = out
        else:
            acc_ref[...] += out
    mlp_copy.wait()
    own, in_part = own_rows(part)
    own_mlp = jnp.where(in_part, mlp_ref[...].astype(jnp.float32), 0.0)
    acc_ref[pl.ds(own, 64), :] = acc_ref[pl.ds(own, 64), :] - own_mlp
    for z in range(4):
        row = pl.multiple_of((z * 2 + core) * group, group)
        mine_ref[z] = acc_ref[pl.ds(row, group), :]
        row = pl.multiple_of((z * 2 + 1 - core) * group, group)
        theirs_ref[z] = acc_ref[pl.ds(row, group), :]


def decode(x, w, mlp, part, after):
    tokens, cols = 512 // PARTS, w.shape[1]
    shape = jax.ShapeDtypeStruct((4, tokens // 8, cols), jnp.float32)
    return pl.pallas_call(
        lambda x_ref, w_ref, m_ref, *refs: decode_kernel(part, x_ref, w_ref, m_ref, *refs[len(after) :]),
        out_shape=(shape, shape),
        in_specs=[VMEM_SPEC, HBM_SPEC, HBM_SPEC] + [ANY_SPEC] * len(after),
        out_specs=(VMEM_SPEC, VMEM_SPEC),
        scratch_shapes=[
            pltpu.VMEM((w.shape[0] // LO, tokens, LO), jnp.bfloat16),
            pltpu.VMEM(w.shape, jnp.bfloat16),
            pltpu.VMEM(mlp.shape, jnp.bfloat16),
            pltpu.VMEM((tokens, cols), jnp.float32),
            pltpu.SemaphoreType.DMA((9,)),
        ],
        compiler_params=PARAMS,
        cost_estimate=pl.CostEstimate(
            flops=4 * tokens * w.shape[0] * cols, transcendentals=0, bytes_accessed=2 * w.size
        ),
    )(x, w, mlp, *after)


def pack_kernel(mine_ref, recv_ref, own_ref, *near_refs):
    z = lax.axis_index("lat") // 2
    own_ref[...] = mine_ref[z] + recv_ref[z]
    for d in (1, 2, 3):
        near_refs[d - 1][...] = encode(mine_ref[z ^ d] + recv_ref[z ^ d])


def pack(mine, recv):
    _, rows, cols = mine.shape
    coded = jax.ShapeDtypeStruct((rows, cols + 128), jnp.int16)
    return pl.pallas_call(
        pack_kernel,
        out_shape=(jax.ShapeDtypeStruct((rows, cols), jnp.float32), coded, coded, coded),
        in_specs=[VMEM_SPEC] * 2,
        out_specs=(VMEM_SPEC,) * 4,
        compiler_params=PARAMS,
    )(mine, recv)


def error_kernel(own_ref, a_ref, b_ref, c_ref, code_ref):
    code_ref[...] = encode(own_ref[...] + decoded(a_ref[...]) + decoded(b_ref[...]) + decoded(c_ref[...]))


def error_of(own, near):
    rows, cols = own.shape
    return pl.pallas_call(
        error_kernel,
        out_shape=jax.ShapeDtypeStruct((rows, cols + 128), jnp.int16),
        in_specs=[VMEM_SPEC] * 4,
        out_specs=VMEM_SPEC,
        compiler_params=PARAMS,
    )(own, *near)


def grads_kernel(part, x_ref, *refs):
    coded = refs[:8]
    w_ref = refs[8]
    first = refs[9 : 9 + 2 * part]
    error_ref, out_ref, err_ref, full_ref = refs[9 + 2 * part :]
    steps = 4
    rows_w = w_ref.shape[0] // steps
    cols = w_ref.shape[1]
    tokens = err_ref.shape[0]
    group = tokens // 8
    lat = lax.axis_index("lat")
    core = lat % 2
    z = lat // 2
    for n, ref in enumerate(coded):
        d, side = n % 4, n // 4
        c = core if side == 0 else 1 - core
        row = pl.multiple_of(((z ^ d) * 2 + c) * group, group)
        e = decoded(ref[...])
        full_ref[pl.ds(row, group), :] = e
        high = e.astype(jnp.bfloat16)
        err_ref[pl.ds(row, group), :cols] = high
        err_ref[pl.ds(row, group), cols:] = (e - high.astype(jnp.float32)).astype(jnp.bfloat16)
    chunks = w_ref.shape[0] // LO
    his = chunks // 2
    width = his * LO
    source = lax.broadcasted_iota(jnp.int32, (16, 128), 1) // 64
    keys, los = [], []
    for i in range(tokens // 16):
        local = x_ref[i, 0:16, :].astype(jnp.int32) - lat * width
        inside = (local >= 0) & (local < width)
        keys.append(jnp.where(inside, (local >> 7) + source * his, -1))
        los.append(local & (LO - 1))
    key = jnp.concatenate(keys, axis=0)
    lo = jnp.concatenate(los, axis=0)
    picked = jnp.zeros((tokens, LO), jnp.float32)
    for i in range(steps):
        w = w_ref[i * rows_w : (i + 1) * rows_w, :]
        grads = lax.dot_general(
            err_ref[...], jnp.concatenate([w, w], axis=1), NT, preferred_element_type=jnp.float32
        )
        for j in range(rows_w // LO):
            found = jnp.take_along_axis(grads[:, j * LO : (j + 1) * LO], lo, axis=1)
            picked = jnp.where(key == i * (rows_w // LO) + j, found, picked)
    own, in_part = own_rows(part)
    error = full_ref[pl.ds(own, 64), :]
    if part == 0:
        error_ref[...] = error
        out_ref[...] = picked
    else:
        error_ref[...] = jnp.where(in_part, error, first[0][...])
        zh = lax.axis_index("tgt") // 16
        out_ref[pl.ds(pl.multiple_of(zh * tokens, tokens), tokens), :] = first[1][...]
        out_ref[pl.ds(pl.multiple_of((1 - zh) * tokens, tokens), tokens), :] = picked


def grads(x, coded, w, part, first, after):
    tokens, cols = 512 // PARTS, w.shape[1]
    args = (x, *coded, w, *first)
    used = len(args)
    return pl.pallas_call(
        lambda *refs: grads_kernel(part, *refs[:used], *refs[used + len(after) :]),
        out_shape=(
            jax.ShapeDtypeStruct((64, cols), jnp.float32),
            jax.ShapeDtypeStruct((tokens * (part + 1), LO), jnp.float32),
        ),
        in_specs=[VMEM_SPEC] * used + [ANY_SPEC] * len(after),
        out_specs=(VMEM_SPEC,) * 2,
        scratch_shapes=[
            pltpu.VMEM((tokens, 2 * cols), jnp.bfloat16),
            pltpu.VMEM((tokens, cols), jnp.float32),
        ],
        compiler_params=PARAMS,
        cost_estimate=pl.CostEstimate(
            flops=4 * tokens * w.shape[0] * cols, transcendentals=0, bytes_accessed=2 * w.size
        ),
    )(*args, *after)


def codes_kernel(index_ref, value_ref, out_ref):
    index = jnp.concatenate([index_ref[0], index_ref[1]], axis=1)
    value = jnp.concatenate([value_ref[0], value_ref[1]], axis=1).astype(jnp.float32) * VALUE_SCALE
    both = jnp.concatenate([index, value.astype(jnp.int32)], axis=0).astype(jnp.int16)
    for i in range(out_ref.shape[0]):
        out_ref[i] = both


def total_kernel(parts_ref, out_ref):
    eight = parts_ref[0:8, :]
    for i in range(1, parts_ref.shape[0] // 8):
        eight = eight + parts_ref[8 * i : 8 * i + 8, :]
    for j in range(2):
        row = eight[j : j + 1] + eight[j + 2 : j + 3] + eight[j + 4 : j + 5] + eight[j + 6 : j + 7]
        row = row * (1.0 / TARGETS)
        for source in range(2):
            out_ref[source, j : j + 1, :] = row[:, source * 64 : (source + 1) * 64]


def shift_z(x, d):
    return lax.ppermute(x, "lat", lat_xor(2 * d))


def layer(code_index, code_value, decoder, mlp_out):
    sources, lat_width, cols = decoder.shape
    w = decoder.reshape(sources * lat_width, cols)
    rows = code_index.shape[1]
    sent = pl.pallas_call(
        codes_kernel,
        out_shape=jax.ShapeDtypeStruct((16, 2 * rows, 128), jnp.int16),
        in_specs=[VMEM_SPEC] * 2,
        out_specs=VMEM_SPEC,
        name="codes",
    )(code_index, code_value)
    groups = [[a * 16 + i for i in range(16)] for a in range(2)]
    x = [lax.all_to_all(sent, "tgt", 0, 0, tiled=True, axis_index_groups=groups)]
    x.append(lax.ppermute(x[0], ("tgt", "lat"), mirror()))

    near_of, own_of, after = [], [], []
    for part in range(PARTS):
        w_hbm = pltpu.with_memory_space_constraint(w, pltpu.HBM)
        mlp_hbm = pltpu.with_memory_space_constraint(mlp_out, pltpu.HBM)
        mine, theirs = decode(x[part], w_hbm, mlp_hbm, part, after)
        recv = lax.ppermute(theirs, "lat", lat_xor(1))
        own_sum, *after = pack(mine, recv)
        own_of.append(own_sum)
        near_of.append([shift_z(after[d - 1], d) for d in (1, 2, 3)])
    coded_of, done = [], ()
    for part in range(PARTS):
        coded = error_of(own_of[part], near_of[part])
        coded_of.append([coded] + [shift_z(coded, d) for d in (1, 2, 3)])
    for part in range(PARTS):
        coded = coded_of[part]
        coded = coded + [lax.ppermute(c, "lat", lat_xor(1)) for c in coded]
        after = [coded_of[-1][0]] if part + 1 < PARTS else []
        done = grads(x[part], coded, w, part, done, after)
    error, picked = done
    parts = lax.all_to_all(picked, ("tgt", "lat"), 0, 0, tiled=True)
    total = pl.pallas_call(
        total_kernel,
        out_shape=jax.ShapeDtypeStruct((sources, 2, 64), jnp.float32),
        in_specs=[VMEM_SPEC],
        out_specs=VMEM_SPEC,
        name="total",
    )(parts)
    return error, total


def solution(mesh):
    placed = (P(None, "tgt", None), P(None, "tgt", None), P(None, "lat", "tgt"), P("lat", "tgt"))
    return jax.shard_map(
        layer,
        mesh=mesh,
        in_specs=placed,
        out_specs=(P("lat", "tgt"), P(None, ("tgt", "lat"), None)),
        check_vma=False,
    )
```

```python
import jax
import jax.numpy as jnp
from jax import lax
from jax.experimental import pallas as pl
from jax.experimental.pallas import tpu as pltpu
from jax.sharding import PartitionSpec as P

TARGETS = 8
PARTS = 2
LO = 128
NT = (((1,), (1,)), ((), ()))
VALUE_SCALE = 256.0
TOP = 32000.0
STEPS = 64.0
VMEM_SPEC = pl.BlockSpec(memory_space=pltpu.VMEM)
ANY_SPEC = pl.BlockSpec(memory_space=pl.ANY)
HBM_SPEC = pl.BlockSpec(memory_space=pltpu.HBM)
PARAMS = pltpu.CompilerParams(vmem_limit_bytes=40 << 20)


def mirror():
    pairs = []
    for t in range(32):
        for i in range(8):
            pairs.append((t * 8 + i, (t ^ 16) * 8 + ((3 - i // 2) * 2 + i % 2)))
    return pairs


def lat_xor(d):
    return [(i, i ^ d) for i in range(8)]


def start_weights(w_hbm, w_ref, sem, steps):
    rows = w_hbm.shape[0] // steps
    copies = []
    for i in range(steps):
        part = pl.ds(i * rows, rows)
        copies.append(pltpu.make_async_copy(w_hbm.at[part], w_ref.at[part], sem.at[i]))
        copies[-1].start()
    return copies


def encode(x):
    cols = x.shape[1] // 128
    parts = [x[:, c * 128 : (c + 1) * 128] for c in range(cols)]
    top = jnp.abs(parts[0])
    for p in parts[1:]:
        top = jnp.maximum(top, jnp.abs(p))
    level = jnp.ceil(jnp.log2(jnp.maximum(top, 1e-30)) * STEPS)
    inverse = jnp.exp2(level * (-1.0 / STEPS)) * TOP
    codes = [jnp.round(p * inverse).astype(jnp.int32).astype(jnp.int16) for p in parts]
    return jnp.concatenate(codes + [level.astype(jnp.int32).astype(jnp.int16)], axis=1)


def decoded(q):
    cols = q.shape[1] // 128 - 1
    wide = q.astype(jnp.int32).astype(jnp.float32)
    scale = jnp.exp2(wide[:, cols * 128 :] * (1.0 / STEPS)) * (1.0 / TOP)
    return jnp.concatenate([wide[:, c * 128 : (c + 1) * 128] * scale for c in range(cols)], axis=1)


def own_rows(part):
    lat = lax.axis_index("lat")
    row = pl.multiple_of((lat // 2 % 2) * 128 + (lat % 2) * 64, 64)
    zh = lax.axis_index("tgt") // 16
    return row, lat // 4 == (zh + part) % 2


def decode_kernel(part, x_ref, w_hbm, mlp_hbm, mine_ref, theirs_ref, codes_ref, w_ref, mlp_ref, acc_ref, sem):
    chunks, tokens = codes_ref.shape[:2]
    his = chunks // 2
    width = his * LO
    group = tokens // 8
    lat = lax.axis_index("lat")
    core = lat % 2
    start = lat * width
    steps = 8
    rows_w = w_hbm.shape[0] // steps
    copies = start_weights(w_hbm, w_ref, sem, steps)
    mlp_copy = pltpu.make_async_copy(mlp_hbm, mlp_ref, sem.at[steps])
    mlp_copy.start()

    half_lane = lax.broadcasted_iota(jnp.int32, (1, 128), 1) < 64
    shape = (his * 8 // 16, 16, 128)
    rows = lax.broadcasted_iota(jnp.int32, shape, 0) * 16 + lax.broadcasted_iota(jnp.int32, shape, 1)
    rows = rows.astype(jnp.float32).astype(jnp.bfloat16)
    zero = jnp.zeros((), jnp.bfloat16)
    one = jnp.ones((), jnp.bfloat16)

    def densify(i, carry):
        block = x_ref[i].astype(jnp.int32)
        local = block[0:16] - start
        inside = (local >= 0) & (local < width)
        hi = jnp.where(inside, (local >> 7) * 8, -1024).astype(jnp.float32)
        lo = (local & (LO - 1)).astype(jnp.float32)
        val = block[16:32].astype(jnp.float32) * (1.0 / VALUE_SCALE)
        both = [(a, pltpu.roll(a, 64, 1)) for a in (hi, lo, val)]

        def pair(n, t, source, extra=None):
            first, second = both[n] if source == 0 else both[n][::-1]
            row = jnp.where(half_lane, first[t : t + 1], second[t + 1 : t + 2])
            if extra is not None:
                row = row + extra
            return jnp.broadcast_to(row, (16, 128)).astype(jnp.bfloat16)[None]

        row = pl.multiple_of(i * 16, 16)
        for source in range(2):
            halves = []
            for t0 in (0, 8):
                lhs, rhs = [], []
                for j in range(4):
                    t = t0 + 2 * j
                    slot = jnp.where(half_lane, 2.0 * j, 2.0 * j + 1)
                    key = pair(0, t, source, slot)
                    lhs.append(jnp.where(rows == key, pair(2, t, source), zero).reshape(his * 8, 128))
                    rhs.append(jnp.where(rows == pair(1, t, source), one, zero).reshape(LO, 128))
                dense = lax.dot_general(
                    jnp.concatenate(lhs, axis=1),
                    jnp.concatenate(rhs, axis=1),
                    NT,
                    preferred_element_type=jnp.float32,
                )
                halves.append(dense.reshape(his, 8, LO))
            dense = jnp.concatenate(halves, axis=1).astype(jnp.bfloat16)
            codes_ref[source * his : (source + 1) * his, pl.ds(row, 16), :] = dense
        return carry

    lax.fori_loop(0, tokens // 16, densify, 0, unroll=8)

    per_step = chunks // steps
    for i in range(steps):
        copies[i].wait()
        lhs = jnp.concatenate([codes_ref[i * per_step + j] for j in range(per_step)], axis=1)
        out = jnp.dot(lhs, w_ref[i * rows_w : (i + 1) * rows_w, :], preferred_element_type=jnp.float32)
        if i == 0:
            acc_ref[...] = out
        else:
            acc_ref[...] += out
    mlp_copy.wait()
    own, in_part = own_rows(part)
    own_mlp = jnp.where(in_part, mlp_ref[...].astype(jnp.float32), 0.0)
    acc_ref[pl.ds(own, 64), :] = acc_ref[pl.ds(own, 64), :] - own_mlp
    for z in range(4):
        row = pl.multiple_of((z * 2 + core) * group, group)
        mine_ref[z] = acc_ref[pl.ds(row, group), :]
        row = pl.multiple_of((z * 2 + 1 - core) * group, group)
        theirs_ref[z] = acc_ref[pl.ds(row, group), :]


def decode(x, w, mlp, part, after):
    tokens, cols = 512 // PARTS, w.shape[1]
    shape = jax.ShapeDtypeStruct((4, tokens // 8, cols), jnp.float32)
    return pl.pallas_call(
        lambda x_ref, w_ref, m_ref, *refs: decode_kernel(part, x_ref, w_ref, m_ref, *refs[len(after) :]),
        out_shape=(shape, shape),
        in_specs=[VMEM_SPEC, HBM_SPEC, HBM_SPEC] + [ANY_SPEC] * len(after),
        out_specs=(VMEM_SPEC, VMEM_SPEC),
        scratch_shapes=[
            pltpu.VMEM((w.shape[0] // LO, tokens, LO), jnp.bfloat16),
            pltpu.VMEM(w.shape, jnp.bfloat16),
            pltpu.VMEM(mlp.shape, jnp.bfloat16),
            pltpu.VMEM((tokens, cols), jnp.float32),
            pltpu.SemaphoreType.DMA((9,)),
        ],
        compiler_params=PARAMS,
        cost_estimate=pl.CostEstimate(
            flops=4 * tokens * w.shape[0] * cols, transcendentals=0, bytes_accessed=2 * w.size
        ),
    )(x, w, mlp, *after)


def pack_kernel(mine_ref, recv_ref, own_ref, *near_refs):
    z = lax.axis_index("lat") // 2
    own_ref[...] = mine_ref[z] + recv_ref[z]
    for d in (1, 2, 3):
        near_refs[d - 1][...] = encode(mine_ref[z ^ d] + recv_ref[z ^ d])


def pack(mine, recv):
    _, rows, cols = mine.shape
    coded = jax.ShapeDtypeStruct((rows, cols + 128), jnp.int16)
    return pl.pallas_call(
        pack_kernel,
        out_shape=(jax.ShapeDtypeStruct((rows, cols), jnp.float32), coded, coded, coded),
        in_specs=[VMEM_SPEC] * 2,
        out_specs=(VMEM_SPEC,) * 4,
        compiler_params=PARAMS,
    )(mine, recv)


def error_kernel(own_ref, a_ref, b_ref, c_ref, code_ref):
    code_ref[...] = encode(own_ref[...] + decoded(a_ref[...]) + decoded(b_ref[...]) + decoded(c_ref[...]))


def error_of(own, near):
    rows, cols = own.shape
    return pl.pallas_call(
        error_kernel,
        out_shape=jax.ShapeDtypeStruct((rows, cols + 128), jnp.int16),
        in_specs=[VMEM_SPEC] * 4,
        out_specs=VMEM_SPEC,
        compiler_params=PARAMS,
    )(own, *near)


def grads_kernel(part, x_ref, *refs):
    coded = refs[:8]
    w_ref = refs[8]
    first = refs[9 : 9 + 2 * part]
    error_ref, out_ref, err_ref, full_ref, rows_ref, sem = refs[9 + 2 * part :]
    steps = 4
    rows_w = w_ref.shape[0] // steps
    cols = w_ref.shape[1]
    tokens = err_ref.shape[0]
    group = tokens // 8
    lat = lax.axis_index("lat")
    core = lat % 2
    z = lat // 2
    for n, ref in enumerate(coded):
        d, side = n % 4, n // 4
        c = core if side == 0 else 1 - core
        row = pl.multiple_of(((z ^ d) * 2 + c) * group, group)
        e = decoded(ref[...])
        full_ref[pl.ds(row, group), :] = e
        high = e.astype(jnp.bfloat16)
        err_ref[pl.ds(row, group), :cols] = high
        err_ref[pl.ds(row, group), cols:] = (e - high.astype(jnp.float32)).astype(jnp.bfloat16)
    own, in_part = own_rows(part)
    rows_ref[...] = full_ref[pl.ds(own, 64), :]
    if part == 1:
        rows_ref[...] = jnp.where(in_part, rows_ref[...], first[0][...])
    error_copy = pltpu.make_async_copy(rows_ref, error_ref, sem)
    error_copy.start()
    chunks = w_ref.shape[0] // LO
    his = chunks // 2
    width = his * LO
    source = lax.broadcasted_iota(jnp.int32, (16, 128), 1) // 64
    keys, los = [], []
    for i in range(tokens // 16):
        local = x_ref[i, 0:16, :].astype(jnp.int32) - lat * width
        inside = (local >= 0) & (local < width)
        keys.append(jnp.where(inside, (local >> 7) + source * his, -1))
        los.append(local & (LO - 1))
    key = jnp.concatenate(keys, axis=0)
    lo = jnp.concatenate(los, axis=0)
    picked = jnp.zeros((tokens, LO), jnp.float32)
    for i in range(steps):
        w = w_ref[i * rows_w : (i + 1) * rows_w, :]
        grads = lax.dot_general(
            err_ref[...], jnp.concatenate([w, w], axis=1), NT, preferred_element_type=jnp.float32
        )
        for j in range(rows_w // LO):
            found = jnp.take_along_axis(grads[:, j * LO : (j + 1) * LO], lo, axis=1)
            picked = jnp.where(key == i * (rows_w // LO) + j, found, picked)
    if part == 0:
        out_ref[...] = picked
    else:
        zh = lax.axis_index("tgt") // 16
        out_ref[pl.ds(pl.multiple_of(zh * tokens, tokens), tokens), :] = first[1][...]
        out_ref[pl.ds(pl.multiple_of((1 - zh) * tokens, tokens), tokens), :] = picked
    error_copy.wait()


def grads(x, coded, w, part, first, after):
    tokens, cols = 512 // PARTS, w.shape[1]
    args = (x, *coded, w, *first)
    used = len(args)
    return pl.pallas_call(
        lambda *refs: grads_kernel(part, *refs[:used], *refs[used + len(after) :]),
        out_shape=(
            jax.ShapeDtypeStruct((64, cols), jnp.float32),
            jax.ShapeDtypeStruct((tokens * (part + 1), LO), jnp.float32),
        ),
        in_specs=[VMEM_SPEC] * used + [ANY_SPEC] * len(after),
        out_specs=(ANY_SPEC, VMEM_SPEC),
        scratch_shapes=[
            pltpu.VMEM((tokens, 2 * cols), jnp.bfloat16),
            pltpu.VMEM((tokens, cols), jnp.float32),
            pltpu.VMEM((64, cols), jnp.float32),
            pltpu.SemaphoreType.DMA,
        ],
        compiler_params=PARAMS,
        cost_estimate=pl.CostEstimate(
            flops=4 * tokens * w.shape[0] * cols, transcendentals=0, bytes_accessed=2 * w.size
        ),
    )(*args, *after)


def codes_kernel(index_ref, value_ref, out_ref):
    index = jnp.concatenate([index_ref[0], index_ref[1]], axis=1)
    value = jnp.concatenate([value_ref[0], value_ref[1]], axis=1).astype(jnp.float32) * VALUE_SCALE
    both = jnp.concatenate([index, value.astype(jnp.int32)], axis=0).astype(jnp.int16)
    for i in range(out_ref.shape[0]):
        out_ref[i] = both


def shift_z(x, d):
    return lax.ppermute(x, "lat", lat_xor(2 * d))


def layer(code_index, code_value, decoder, mlp_out):
    sources, lat_width, cols = decoder.shape
    w = decoder.reshape(sources * lat_width, cols)
    rows = code_index.shape[1]
    sent = pl.pallas_call(
        codes_kernel,
        out_shape=jax.ShapeDtypeStruct((16, 2 * rows, 128), jnp.int16),
        in_specs=[VMEM_SPEC] * 2,
        out_specs=VMEM_SPEC,
        name="codes",
    )(code_index, code_value)
    groups = [[a * 16 + i for i in range(16)] for a in range(2)]
    x = [lax.all_to_all(sent, "tgt", 0, 0, tiled=True, axis_index_groups=groups)]
    x.append(lax.ppermute(x[0], ("tgt", "lat"), mirror()))

    near_of, own_of, after = [], [], []
    for part in range(PARTS):
        w_hbm = pltpu.with_memory_space_constraint(w, pltpu.HBM)
        mlp_hbm = pltpu.with_memory_space_constraint(mlp_out, pltpu.HBM)
        mine, theirs = decode(x[part], w_hbm, mlp_hbm, part, after)
        recv = lax.ppermute(theirs, "lat", lat_xor(1))
        own_sum, *after = pack(mine, recv)
        own_of.append(own_sum)
        near_of.append([shift_z(after[d - 1], d) for d in (1, 2, 3)])
    coded_of, done = [], ()
    for part in range(PARTS):
        coded = error_of(own_of[part], near_of[part])
        coded_of.append([coded] + [shift_z(coded, d) for d in (1, 2, 3)])
    for part in range(PARTS):
        coded = coded_of[part]
        coded = coded + [lax.ppermute(c, "lat", lat_xor(1)) for c in coded]
        after = [coded_of[-1][0]] if part + 1 < PARTS else []
        done = grads(x[part], coded, w, part, done, after)
    error, picked = done
    parts = lax.all_to_all(picked, ("tgt", "lat"), 0, 0, tiled=True)
    total = jnp.sum(parts.reshape(256, 2, sources, 64), axis=0)
    return error, jnp.transpose(total, (1, 0, 2)) / TARGETS


def solution(mesh):
    placed = (P(None, "tgt", None), P(None, "tgt", None), P(None, "lat", "tgt"), P("lat", "tgt"))
    return jax.shard_map(
        layer,
        mesh=mesh,
        in_specs=placed,
        out_specs=(P("lat", "tgt"), P(None, ("tgt", "lat"), None)),
        check_vma=False,
    )
```

```python
import jax
import jax.numpy as jnp
from jax import lax
from jax.experimental import pallas as pl
from jax.experimental.pallas import tpu as pltpu
from jax.sharding import PartitionSpec as P

TARGETS = 8
PARTS = 2
LO = 128
NT = (((1,), (1,)), ((), ()))
VALUE_SCALE = 256.0
TOP = 32000.0
STEPS = 64.0
VMEM_SPEC = pl.BlockSpec(memory_space=pltpu.VMEM)
ANY_SPEC = pl.BlockSpec(memory_space=pl.ANY)
HBM_SPEC = pl.BlockSpec(memory_space=pltpu.HBM)
PARAMS = pltpu.CompilerParams(vmem_limit_bytes=40 << 20)


def mirror():
    pairs = []
    for t in range(32):
        for i in range(8):
            pairs.append((t * 8 + i, (t ^ 16) * 8 + ((3 - i // 2) * 2 + i % 2)))
    return pairs


def lat_xor(d):
    return [(i, i ^ d) for i in range(8)]


def start_weights(w_hbm, w_ref, sem, steps):
    rows = w_hbm.shape[0] // steps
    copies = []
    for i in range(steps):
        part = pl.ds(i * rows, rows)
        copies.append(pltpu.make_async_copy(w_hbm.at[part], w_ref.at[part], sem.at[i]))
        copies[-1].start()
    return copies


def encode(x):
    cols = x.shape[1] // 128
    half = x.shape[0] // 2
    parts = [x[:, c * 128 : (c + 1) * 128] for c in range(cols)]
    top = jnp.abs(parts[0])
    for p in parts[1:]:
        top = jnp.maximum(top, jnp.abs(p))
    top = jnp.maximum(top[:half], top[half:])
    level = jnp.ceil(jnp.log2(jnp.maximum(top, 1e-30)) * STEPS)
    inverse = jnp.exp2(level * (-1.0 / STEPS)) * TOP
    inverse = jnp.concatenate([inverse, inverse], axis=0)
    codes = [jnp.round(p * inverse).astype(jnp.int32).astype(jnp.int16) for p in parts]
    return jnp.concatenate(codes + [level.astype(jnp.int32).astype(jnp.int16)], axis=0)


def coded_shape(rows, cols):
    return jax.ShapeDtypeStruct((rows * (cols // 128) + rows // 2, 128), jnp.int16)


def decoded(q, rows):
    cols = q.shape[0] // rows
    wide = q.astype(jnp.int32).astype(jnp.float32)
    scale = jnp.exp2(wide[cols * rows :] * (1.0 / STEPS)) * (1.0 / TOP)
    scale = jnp.concatenate([scale, scale], axis=0)
    return jnp.concatenate([wide[c * rows : (c + 1) * rows] * scale for c in range(cols)], axis=1)


def own_rows(part):
    lat = lax.axis_index("lat")
    row = pl.multiple_of((lat // 2 % 2) * 128 + (lat % 2) * 64, 64)
    zh = lax.axis_index("tgt") // 16
    return row, lat // 4 == (zh + part) % 2


def decode_kernel(part, x_ref, w_hbm, mlp_hbm, mine_ref, theirs_ref, codes_ref, w_ref, mlp_ref, acc_ref, sem):
    chunks, tokens = codes_ref.shape[:2]
    his = chunks // 2
    width = his * LO
    group = tokens // 8
    lat = lax.axis_index("lat")
    core = lat % 2
    start = lat * width
    steps = 2
    rows_w = w_hbm.shape[0] // steps
    copies = start_weights(w_hbm, w_ref, sem, steps)
    mlp_copy = pltpu.make_async_copy(mlp_hbm, mlp_ref, sem.at[steps])
    mlp_copy.start()

    half_lane = lax.broadcasted_iota(jnp.int32, (1, 128), 1) < 64
    shape = (his * 8 // 16, 16, 128)
    rows = lax.broadcasted_iota(jnp.int32, shape, 0) * 16 + lax.broadcasted_iota(jnp.int32, shape, 1)
    rows = rows.astype(jnp.float32).astype(jnp.bfloat16)
    zero = jnp.zeros((), jnp.bfloat16)
    one = jnp.ones((), jnp.bfloat16)

    def densify(i, carry):
        block = x_ref[i].astype(jnp.int32)
        local = block[0:16] - start
        inside = (local >= 0) & (local < width)
        hi = jnp.where(inside, (local >> 7) * 8, -1024).astype(jnp.float32)
        lo = (local & (LO - 1)).astype(jnp.float32)
        val = block[16:32].astype(jnp.float32) * (1.0 / VALUE_SCALE)
        both = [(a, pltpu.roll(a, 64, 1)) for a in (hi, lo, val)]

        def pair(n, t, source, extra=None):
            first, second = both[n] if source == 0 else both[n][::-1]
            row = jnp.where(half_lane, first[t : t + 1], second[t + 1 : t + 2])
            if extra is not None:
                row = row + extra
            return jnp.broadcast_to(row, (16, 128)).astype(jnp.bfloat16)[None]

        row = pl.multiple_of(i * 16, 16)
        for source in range(2):
            halves = []
            for t0 in (0, 8):
                lhs, rhs = [], []
                for j in range(4):
                    t = t0 + 2 * j
                    slot = jnp.where(half_lane, 2.0 * j, 2.0 * j + 1)
                    key = pair(0, t, source, slot)
                    lhs.append(jnp.where(rows == key, pair(2, t, source), zero).reshape(his * 8, 128))
                    rhs.append(jnp.where(rows == pair(1, t, source), one, zero).reshape(LO, 128))
                dense = lax.dot_general(
                    jnp.concatenate(lhs, axis=1),
                    jnp.concatenate(rhs, axis=1),
                    NT,
                    preferred_element_type=jnp.float32,
                )
                halves.append(dense.reshape(his, 8, LO))
            dense = jnp.concatenate(halves, axis=1).astype(jnp.bfloat16)
            codes_ref[source * his : (source + 1) * his, pl.ds(row, 16), :] = dense
        return carry

    lax.fori_loop(0, tokens // 16, densify, 0, unroll=8)

    per_step = chunks // steps
    for i in range(steps):
        copies[i].wait()
        lhs = jnp.concatenate([codes_ref[i * per_step + j] for j in range(per_step)], axis=1)
        out = jnp.dot(lhs, w_ref[i * rows_w : (i + 1) * rows_w, :], preferred_element_type=jnp.float32)
        if i == 0:
            acc_ref[...] = out
        else:
            acc_ref[...] += out
    mlp_copy.wait()
    own, in_part = own_rows(part)
    own_mlp = jnp.where(in_part, mlp_ref[...].astype(jnp.float32), 0.0)
    acc_ref[pl.ds(own, 64), :] = acc_ref[pl.ds(own, 64), :] - own_mlp
    for z in range(4):
        row = pl.multiple_of((z * 2 + core) * group, group)
        mine_ref[z] = acc_ref[pl.ds(row, group), :]
        row = pl.multiple_of((z * 2 + 1 - core) * group, group)
        theirs_ref[z] = acc_ref[pl.ds(row, group), :]


def decode(x, w, mlp, part, after):
    tokens, cols = 512 // PARTS, w.shape[1]
    shape = jax.ShapeDtypeStruct((4, tokens // 8, cols), jnp.float32)
    return pl.pallas_call(
        lambda x_ref, w_ref, m_ref, *refs: decode_kernel(part, x_ref, w_ref, m_ref, *refs[len(after) :]),
        out_shape=(shape, shape),
        in_specs=[VMEM_SPEC, HBM_SPEC, HBM_SPEC] + [ANY_SPEC] * len(after),
        out_specs=(VMEM_SPEC, VMEM_SPEC),
        scratch_shapes=[
            pltpu.VMEM((w.shape[0] // LO, tokens, LO), jnp.bfloat16),
            pltpu.VMEM(w.shape, jnp.bfloat16),
            pltpu.VMEM(mlp.shape, jnp.bfloat16),
            pltpu.VMEM((tokens, cols), jnp.float32),
            pltpu.SemaphoreType.DMA((9,)),
        ],
        compiler_params=PARAMS,
        cost_estimate=pl.CostEstimate(
            flops=4 * tokens * w.shape[0] * cols, transcendentals=0, bytes_accessed=2 * w.size
        ),
    )(x, w, mlp, *after)


def pack_kernel(mine_ref, recv_ref, own_ref, *near_refs):
    z = lax.axis_index("lat") // 2
    own_ref[...] = mine_ref[z] + recv_ref[z]
    for d in (1, 2, 3):
        near_refs[d - 1][...] = encode(mine_ref[z ^ d] + recv_ref[z ^ d])


def pack(mine, recv):
    _, rows, cols = mine.shape
    coded = coded_shape(rows, cols)
    return pl.pallas_call(
        pack_kernel,
        out_shape=(jax.ShapeDtypeStruct((rows, cols), jnp.float32), coded, coded, coded),
        in_specs=[VMEM_SPEC] * 2,
        out_specs=(VMEM_SPEC,) * 4,
        compiler_params=PARAMS,
    )(mine, recv)


def error_kernel(own_ref, a_ref, b_ref, c_ref, code_ref):
    rows = own_ref.shape[0]
    total = own_ref[...] + decoded(a_ref[...], rows) + decoded(b_ref[...], rows)
    code_ref[...] = encode(total + decoded(c_ref[...], rows))


def error_of(own, near):
    rows, cols = own.shape
    return pl.pallas_call(
        error_kernel,
        out_shape=coded_shape(rows, cols),
        in_specs=[VMEM_SPEC] * 4,
        out_specs=VMEM_SPEC,
        compiler_params=PARAMS,
    )(own, *near)


def grads_kernel(part, x_ref, *refs):
    coded = refs[:8]
    w_ref = refs[8]
    first = refs[9 : 9 + 2 * part]
    error_ref, out_ref, err_ref, full_ref = refs[9 + 2 * part :]
    steps = 4
    rows_w = w_ref.shape[0] // steps
    cols = w_ref.shape[1]
    tokens = err_ref.shape[0]
    group = tokens // 8
    lat = lax.axis_index("lat")
    core = lat % 2
    z = lat // 2
    for n, ref in enumerate(coded):
        d, side = n % 4, n // 4
        c = core if side == 0 else 1 - core
        row = pl.multiple_of(((z ^ d) * 2 + c) * group, group)
        e = decoded(ref[...], group)
        full_ref[pl.ds(row, group), :] = e
        high = e.astype(jnp.bfloat16)
        err_ref[pl.ds(row, group), :cols] = high
        err_ref[pl.ds(row, group), cols:] = (e - high.astype(jnp.float32)).astype(jnp.bfloat16)
    chunks = w_ref.shape[0] // LO
    his = chunks // 2
    width = his * LO
    source = lax.broadcasted_iota(jnp.int32, (16, 128), 1) // 64
    keys, los = [], []
    for i in range(tokens // 16):
        local = x_ref[i, 0:16, :].astype(jnp.int32) - lat * width
        inside = (local >= 0) & (local < width)
        keys.append(jnp.where(inside, (local >> 7) + source * his, -1))
        los.append(local & (LO - 1))
    key = jnp.concatenate(keys, axis=0)
    lo = jnp.concatenate(los, axis=0)
    picked = jnp.zeros((tokens, LO), jnp.float32)
    for i in range(steps):
        w = w_ref[i * rows_w : (i + 1) * rows_w, :]
        grads = lax.dot_general(
            err_ref[...], jnp.concatenate([w, w], axis=1), NT, preferred_element_type=jnp.float32
        )
        for j in range(rows_w // LO):
            found = jnp.take_along_axis(grads[:, j * LO : (j + 1) * LO], lo, axis=1)
            picked = jnp.where(key == i * (rows_w // LO) + j, found, picked)
    own, in_part = own_rows(part)
    error = full_ref[pl.ds(own, 64), :]
    if part == 0:
        error_ref[...] = error
        out_ref[...] = picked
    else:
        error_ref[...] = jnp.where(in_part, error, first[0][...])
        zh = lax.axis_index("tgt") // 16
        out_ref[pl.ds(pl.multiple_of(zh * tokens, tokens), tokens), :] = first[1][...]
        out_ref[pl.ds(pl.multiple_of((1 - zh) * tokens, tokens), tokens), :] = picked


def grads(x, coded, w, part, first, after):
    tokens, cols = 512 // PARTS, w.shape[1]
    args = (x, *coded, w, *first)
    used = len(args)
    return pl.pallas_call(
        lambda *refs: grads_kernel(part, *refs[:used], *refs[used + len(after) :]),
        out_shape=(
            jax.ShapeDtypeStruct((64, cols), jnp.float32),
            jax.ShapeDtypeStruct((tokens * (part + 1), LO), jnp.float32),
        ),
        in_specs=[VMEM_SPEC] * used + [ANY_SPEC] * len(after),
        out_specs=(VMEM_SPEC,) * 2,
        scratch_shapes=[
            pltpu.VMEM((tokens, 2 * cols), jnp.bfloat16),
            pltpu.VMEM((tokens, cols), jnp.float32),
        ],
        compiler_params=PARAMS,
        cost_estimate=pl.CostEstimate(
            flops=4 * tokens * w.shape[0] * cols, transcendentals=0, bytes_accessed=2 * w.size
        ),
    )(*args, *after)


def codes_kernel(index_ref, value_ref, out_ref):
    index = jnp.concatenate([index_ref[0], index_ref[1]], axis=1)
    value = jnp.concatenate([value_ref[0], value_ref[1]], axis=1).astype(jnp.float32) * VALUE_SCALE
    both = jnp.concatenate([index, value.astype(jnp.int32)], axis=0).astype(jnp.int16)
    for i in range(out_ref.shape[0]):
        out_ref[i] = both


def shift_z(x, d):
    return lax.ppermute(x, "lat", lat_xor(2 * d))


def layer(code_index, code_value, decoder, mlp_out):
    sources, lat_width, cols = decoder.shape
    w = decoder.reshape(sources * lat_width, cols)
    rows = code_index.shape[1]
    sent = pl.pallas_call(
        codes_kernel,
        out_shape=jax.ShapeDtypeStruct((16, 2 * rows, 128), jnp.int16),
        in_specs=[VMEM_SPEC] * 2,
        out_specs=VMEM_SPEC,
        name="codes",
    )(code_index, code_value)
    groups = [[a * 16 + i for i in range(16)] for a in range(2)]
    x = [lax.all_to_all(sent, "tgt", 0, 0, tiled=True, axis_index_groups=groups)]
    x.append(lax.ppermute(x[0], ("tgt", "lat"), mirror()))

    near_of, own_of, after = [], [], []
    for part in range(PARTS):
        w_hbm = pltpu.with_memory_space_constraint(w, pltpu.HBM)
        mlp_hbm = pltpu.with_memory_space_constraint(mlp_out, pltpu.HBM)
        mine, theirs = decode(x[part], w_hbm, mlp_hbm, part, after)
        recv = lax.ppermute(theirs, "lat", lat_xor(1))
        own_sum, *after = pack(mine, recv)
        own_of.append(own_sum)
        near_of.append([shift_z(after[d - 1], d) for d in (1, 2, 3)])
    coded_of, done = [], ()
    for part in range(PARTS):
        coded = error_of(own_of[part], near_of[part])
        coded_of.append([coded] + [shift_z(coded, d) for d in (1, 2, 3)])
    for part in range(PARTS):
        coded = coded_of[part]
        coded = coded + [lax.ppermute(c, "lat", lat_xor(1)) for c in coded]
        after = [coded_of[-1][0]] if part + 1 < PARTS else []
        done = grads(x[part], coded, w, part, done, after)
    error, picked = done
    parts = lax.all_to_all(picked, ("tgt", "lat"), 0, 0, tiled=True)
    total = jnp.sum(parts.reshape(256, 2, sources, 64), axis=0)
    return error, jnp.transpose(total, (1, 0, 2)) / TARGETS


def solution(mesh):
    placed = (P(None, "tgt", None), P(None, "tgt", None), P(None, "lat", "tgt"), P("lat", "tgt"))
    return jax.shard_map(
        layer,
        mesh=mesh,
        in_specs=placed,
        out_specs=(P("lat", "tgt"), P(None, ("tgt", "lat"), None)),
        check_vma=False,
    )
```
